512 devices in a mesh: ens: 8 (over z_hi, core), grid: 64 (over x, z_lo, y).
Axes of the slice: x: 4, y: 4, z: 16 (z_hi: 4, z_lo: 4; z = z_hi * 4 + z_lo), core: 2. Of those that a mesh axis runs over, the one named last changes fastest.
Arguments:
- states: bfloat16 [16, 16384, 1024], P('ens', 'grid'), may hold values from -4 to 4
- gain: float32 [1024], replicated, may hold values from 0.1 to 1.9
- w_query: bfloat16 [1024, 512], P('grid'), may hold values from -1 to 1
- w_keyval: bfloat16 [1024, 1024], P('grid'), may hold values from -1 to 1
- w_out: bfloat16 [512, 1024], P('grid'), may hold values from -0.75 to 0.75
- w_decode: bfloat16 [100, 1024], replicated, may hold values from -0.1875 to 0.1875
- neighbours: int32 [128, 4], P('grid'), may hold values from 0 to 127, as said below
- counts: int32 [128], P('grid'), may hold values from 1 to 4, as said below
- targets: bfloat16 [100, 16384], P(None, 'grid'), may hold values from -5 to 5
Outputs:
- gradient: bfloat16 [100, 16, 16384], P(None, 'ens', 'grid')
The draws below stay inside these ranges and needn't reach their ends.
Inputs may be any that keep to these rules, and one draw needn't show every extreme that they name: `neighbours`: the 4 entries of a block's row are distinct blocks within 2 blocks of it in the cyclic order of blocks (block 127 is next to block 0); entries beyond the row's count are padding of the same kind. `counts`: block 0 uses all 4 slots.
All inputs are finite; a program needn't handle non-finite values.
Results may differ from the reference program's by a relative error of at most 0.011.
Values may be sent and summed in bfloat16 or wider, within the bound.
No kernel may reach another device: no remote copies, remote signals or barrier semaphores. Data moves between devices by JAX's collectives and lax.ppermute only.
A program may use at most 64 MiB of HBM per device.

```python
import math
import jax
import jax.numpy as jnp
from jax import lax

D = 1024
HEADS = 8
HD = 64
HW = 512
FIELDS = 100
MEMBERS = 16
P_DEV = 256
POINTS = 16384
BLK = 128
NB = 4
REACH = 2
NBLK = 128


def draw_neighbours(key, part):
    choices_total = 2 * REACH + 1
    scores = jax.random.randint(jax.random.fold_in(key, 11), (NBLK, choices_total), 0, 4096) * choices_total
    scores = scores + jnp.arange(choices_total, dtype=jnp.int32)[None, :]
    picked_scores, order = lax.top_k(scores, NB)
    offsets = order.astype(jnp.int32) - REACH
    return ((jnp.arange(NBLK, dtype=jnp.int32)[:, None] + offsets) % NBLK).astype(jnp.int32)


def draw_counts(key, part):
    drawn = jax.random.randint(jax.random.fold_in(key, 23), (NBLK,), 1, NB + 1).astype(jnp.int32)
    return drawn.at[0].set(NB)


def shared_signs(key, salt, length):
    bits = jax.random.randint(jax.random.fold_in(key, salt), (length,), 0, 2)
    return (bits * 2 - 1).astype(jnp.float32)


def drawn_columns(key):
    direction = shared_signs(key, 101, D)
    head_signs = shared_signs(key, 103, HEADS * HD)
    ranking = jax.random.permutation(jax.random.fold_in(key, 107), HEADS).astype(jnp.float32)
    strength = 170.0 + 230.0 * ranking / max(HEADS - 1, 1)
    factor = jnp.sqrt(strength / math.sqrt(HD)) / D
    columns = jnp.repeat(factor, HD) * head_signs
    return direction[:, None] * columns[None, :]


def draw_w_query(key, part):
    planted = drawn_columns(key)
    drawn = jax.random.normal(jax.random.fold_in(key, 31), (D, HEADS * HD), jnp.float32)
    base = jnp.clip(drawn, -6.0, 6.0) / math.sqrt(D)
    return (base + planted).astype(jnp.bfloat16)


def draw_w_keyval(key, part):
    planted = drawn_columns(key)
    widened = jnp.concatenate([planted, jnp.zeros((D, HEADS * HD), jnp.float32)], axis=1)
    drawn = jax.random.normal(jax.random.fold_in(key, 37), (D, 2 * HEADS * HD), jnp.float32)
    base = jnp.clip(drawn, -6.0, 6.0) / math.sqrt(D)
    return (base + widened).astype(jnp.bfloat16)


def draw_states(key, part):
    direction = shared_signs(key, 101, D)
    picked_block = jax.random.randint(jax.random.fold_in(key, 41), (MEMBERS, NBLK, 1), 0, 8) == 0
    picked_point = jax.random.randint(jax.random.fold_in(key, 43), (MEMBERS, NBLK, BLK), 0, BLK) < 4
    planted = jnp.logical_and(picked_block, picked_point).reshape(MEMBERS, POINTS, 1)
    amplitude = jax.random.uniform(jax.random.fold_in(key, 47), (MEMBERS, POINTS, 1), jnp.float32, 1.3, 2.0)
    noise = jax.random.normal(jax.random.fold_in(key, 53), (MEMBERS, POINTS, D), jnp.float32)
    entries = jnp.clip(0.5 * noise, -4.0, 4.0)
    aligned = amplitude * direction + jnp.clip(noise, -2.0, 2.0)
    return jnp.where(planted, aligned, entries).astype(jnp.bfloat16)


def levels(stream_key, dims, cuts, least, high):
    def one(axis_at, blocks):
        steps = jax.random.uniform(jax.random.fold_in(jax.random.fold_in(stream_key, 6), axis_at), (blocks,), jnp.float32, least / len(cuts), high / len(cuts))
        return jnp.repeat(jnp.exp(steps), dims[axis_at] // blocks).reshape((-1,) + (1,) * (len(dims) - axis_at - 1))

    factor_of = one(*cuts[0])
    for cut in cuts[1:]:
        factor_of = factor_of * one(*cut)
    return factor_of


def gaussian(rng, shape, width, most, shards=(), kind=jnp.bfloat16):
    level = levels(rng, shape, shards, -0.22, 0.18) if shards else 1.0
    values = jax.random.normal(rng, shape, jnp.float32) * width * level
    return jnp.minimum(jnp.maximum(values, -most), most).astype(kind)


def setup_inputs(seed: int = 0) -> dict:
    splits = jax.random.split(jax.random.key(seed), 10)
    return {
        "states": draw_states(jax.random.fold_in(splits[9], 71), 0),
        "gain": jnp.clip(1.0 + 0.18 * jax.random.normal(splits[1], (D,), jnp.float32), 0.1, 1.9),
        "w_query": draw_w_query(jax.random.fold_in(splits[9], 71), 0),
        "w_keyval": draw_w_keyval(jax.random.fold_in(splits[9], 71), 0),
        "w_out": gaussian(splits[4], (HW, D), HD ** -0.5, 0.75, ((0, 64),)),
        "w_decode": gaussian(splits[5], (FIELDS, D), D ** -0.5, 0.1875),
        "neighbours": draw_neighbours(jax.random.fold_in(splits[9], 71), 0),
        "counts": draw_counts(jax.random.fold_in(splits[9], 71), 0),
        "targets": gaussian(splits[8], (FIELDS, POINTS), 1.0, 5.0, ((1, 64),)),
    }


alpha_fair = 0.95
smoothing = 0.25

def layer_norm(states, gain):
    widened = states.astype(jnp.float32)
    centred = widened - lax.optimization_barrier(jnp.mean(widened, axis=-1, keepdims=True))
    spread = lax.optimization_barrier(jnp.mean(centred * centred, axis=-1, keepdims=True))
    return (centred * lax.rsqrt(spread + 1e-05) * gain.astype(jnp.float32)).astype(jnp.bfloat16)

def attend(queries, key_rows, value_rows, usable):
    heads_q = queries.reshape(queries.shape[0], HEADS, HD).astype(jnp.float32)
    heads_k = key_rows.reshape(key_rows.shape[0], HEADS, HD).astype(jnp.float32)
    heads_v = value_rows.reshape(value_rows.shape[0], HEADS, HD).astype(jnp.float32)
    scores = jnp.einsum('qhd,khd->hqk', heads_q, heads_k) / math.sqrt(HD)
    scores = jnp.where(usable[None, None, :], scores, -1e+30)
    largest = lax.optimization_barrier(jnp.max(scores, axis=-1, keepdims=True))
    expanded = jnp.where(usable[None, None, :], jnp.exp(scores - largest), 0.0)
    weights = (expanded / lax.optimization_barrier(jnp.sum(expanded, axis=-1, keepdims=True))).astype(jnp.bfloat16)
    mixed = jnp.einsum('hqk,khd->qhd', weights.astype(jnp.float32), heads_v)
    return mixed.reshape(queries.shape[0], HEADS * HD).astype(jnp.bfloat16)

def smooth_sign(difference):
    return difference * lax.rsqrt(difference * difference + smoothing * smoothing)

def reference(states, gain, w_query, w_keyval, w_out, w_decode, neighbours, counts, targets):
    head_cols = HEADS * HD
    block_count = P_DEV // BLK
    group_total = NBLK // block_count
    neighbour_groups = neighbours.reshape(group_total, block_count, NB)
    count_groups = counts.reshape(group_total, block_count)

    def member_layer(member_state):
        normed = layer_norm(member_state, gain)
        queries = jnp.dot(normed, w_query, preferred_element_type=jnp.float32).astype(jnp.bfloat16)
        keyval = jnp.dot(normed, w_keyval, preferred_element_type=jnp.float32).astype(jnp.bfloat16)
        keyval_blocks = keyval.reshape(NBLK, BLK, 2 * head_cols)
        query_groups = queries.reshape(group_total, block_count, BLK, head_cols)

        def block_group(pieces):
            query_part, neighbour_part, count_part = pieces
            picked = keyval_blocks[neighbour_part].reshape(block_count, NB * BLK, 2 * head_cols)
            usable = jnp.repeat(jnp.arange(NB)[None, :] < count_part[:, None], BLK, axis=1)
            return jax.vmap(attend)(query_part, picked[..., :head_cols], picked[..., head_cols:], usable)
        attended = lax.map(block_group, (query_groups, neighbour_groups, count_groups))
        attended = attended.reshape(POINTS, head_cols)
        updated = (member_state.astype(jnp.float32) + jnp.dot(attended, w_out, preferred_element_type=jnp.float32)).astype(jnp.bfloat16)
        return jnp.dot(w_decode, updated.T, preferred_element_type=jnp.float32).astype(jnp.bfloat16)
    predicted = jnp.transpose(lax.map(member_layer, states), (1, 0, 2))
    member_values = predicted.astype(jnp.float32)
    own_term = smooth_sign(member_values - targets.astype(jnp.float32)[:, None, :])

    def add_member(index, pair_sum):
        other = lax.dynamic_slice_in_dim(member_values, jnp.asarray(index).astype(jnp.int32), 1, 1)
        return pair_sum + smooth_sign(member_values - other)
    pair_sum = lax.fori_loop(0, MEMBERS, add_member, jnp.zeros_like(member_values))
    pair_weight = (1.0 - (1.0 - alpha_fair) / MEMBERS) / (MEMBERS - 1)
    return (own_term - pair_weight * pair_sum).astype(jnp.bfloat16)
```

```python
import functools

import jax
import jax.numpy as jnp
from jax import lax
from jax.experimental import pallas as pl
from jax.experimental.pallas import tpu as pltpu
from jax.sharding import PartitionSpec as P

HEADS = 8
HD = 64
BLK = 128
NB = 4
REACH = 2
HW = HEADS * HD

alpha_fair = 0.95
smoothing = 0.25


BOTH = ("ens", "grid")


def place_of(index):
    ens, grid = divmod(index, 64)
    return grid // 16, grid % 4, (ens // 2) * 4 + (grid // 4) % 4, ens % 2


def index_of(x, y, z, core):
    return ((z // 4) * 2 + core) * 64 + (x % 4) * 16 + (z % 4) * 4 + y % 4


def source_along(axis, step, x, y, z, core):
    if axis == "x":
        return index_of(x + step, y, z, core)
    if axis == "y":
        return index_of(x, y + step, z, core)
    if step == 3 or (step == 2 and z % 2):
        step = step - 4
    return index_of(x, y, (z + step) % 16, core)


def shift(array, axes, step):
    perm = []
    for target in range(512):
        x, y, z, core = place_of(target)
        perm.append((source_along(axes[core], step, x, y, z, core), target))
    return lax.ppermute(array, BOTH, perm)


def swap_cores(array):
    return lax.ppermute(array, "ens", [(i, i ^ 1) for i in range(8)])


def norm_kernel(states_ref, gain_ref, out_ref):
    widened = states_ref[...].astype(jnp.float32)
    centred = widened - jnp.mean(widened, axis=-1, keepdims=True)
    spread = jnp.mean(centred * centred, axis=-1, keepdims=True)
    out_ref[...] = (centred * lax.rsqrt(spread + 1e-05) * gain_ref[...]).astype(jnp.bfloat16)


def layer_norm(states, gain):
    rows, features = states.shape
    tile = 128
    return pl.pallas_call(
        norm_kernel,
        out_shape=jax.ShapeDtypeStruct((rows, features), jnp.bfloat16),
        grid=(rows // tile,),
        in_specs=[
            pl.BlockSpec((tile, features), lambda i: (i, 0)),
            pl.BlockSpec((1, features), lambda i: (0, 0)),
        ],
        out_specs=pl.BlockSpec((tile, features), lambda i: (i, 0)),
        name="norm",
    )(states, gain.reshape(1, features))


def assemble(place_ref, first, second, wqk_ref, wv_ref, wo_ref):
    x0, z0 = place_ref[0], place_ref[1]
    for far in range(4):
        for near in range(4):
            row = pl.multiple_of(((x0 + far) % 4) * 256 + ((z0 + near) % 4) * 64, 64)
            wqk_ref[pl.ds(row, 64), :] = first[far][near]
            row = pl.multiple_of(((x0 + near) % 4) * 256 + ((z0 + far) % 4) * 64, 64)
            wv_ref[pl.ds(row, 64), :] = second[far][near, :, :HW]
            half = pl.multiple_of(((x0 + near) % 4) * 128 + ((z0 + far) % 4) * 32, 32)
            wo_ref[pl.ds(half, 32), :HW] = second[far][near, :32, HW:]
            wo_ref[pl.ds(half, 32), HW:] = second[far][near, 32:, HW:]


def main_kernel(
    place_ref, ids_ref, counts_ref,
    own_ref, low_ref, high_ref, states_ref, decode_ref,
    a0, a1, a2, a3, b0, b1, b2, b3,
    out_ref,
    wqk_ref, wv_ref, wo_ref, keys_ref, values_ref, query_ref, attended_ref,
):
    mine, other = (a0, a1, a2, a3), (b0, b1, b2, b3)

    @pl.when(place_ref[2] == 0)
    def _():
        assemble(place_ref, mine, other, wqk_ref, wv_ref, wo_ref)

    @pl.when(place_ref[2] == 1)
    def _():
        assemble(place_ref, other, mine, wqk_ref, wv_ref, wo_ref)

    members = own_ref.shape[0]
    lane = lax.broadcasted_iota(jnp.int32, (BLK, 4 * HD), 1) // HD
    for member in range(members):
        for at, source in enumerate((low_ref, own_ref, high_ref)):
            rows = source[member]
            for blocks, weights in ((keys_ref, wqk_ref[:, HW:]), (values_ref, wv_ref[...])):
                product = jnp.dot(rows, weights, preferred_element_type=jnp.float32)
                product = product.astype(jnp.bfloat16)
                blocks[2 * at] = product[:BLK]
                blocks[2 * at + 1] = product[BLK:]
        query = jnp.dot(own_ref[member], wqk_ref[:, :HW], preferred_element_type=jnp.float32)
        query_ref[...] = query.astype(jnp.bfloat16) * jnp.bfloat16(0.125)
        for block in range(2):
            for group in range(2):
                columns = slice(group * 4 * HD, (group + 1) * 4 * HD)
                part = query_ref[block * BLK : (block + 1) * BLK, columns]
                zero = jnp.zeros_like(part)
                stacked = jnp.concatenate(
                    [jnp.where(lane == head, part, zero) for head in range(4)], axis=0
                )
                scores = []
                for slot in range(NB):
                    block_keys = keys_ref[ids_ref[block * NB + slot], :, columns]
                    raw = lax.dot_general(
                        stacked, block_keys, (((1,), (1,)), ((), ())),
                        preferred_element_type=jnp.float32,
                    )
                    if slot:
                        raw = jnp.where(slot < counts_ref[block], raw, -1e30)
                    scores.append(raw)
                top = functools.reduce(jnp.maximum, scores)
                top = jnp.max(top, axis=-1, keepdims=True)
                expanded = [jnp.exp(raw - top) for raw in scores]
                total = jnp.sum(functools.reduce(jnp.add, expanded), axis=-1, keepdims=True)
                scale = 1.0 / total
                mixed = None
                for slot in range(NB):
                    block_values = values_ref[ids_ref[block * NB + slot], :, columns]
                    term = jnp.dot(
                        (expanded[slot] * scale).astype(jnp.bfloat16), block_values,
                        preferred_element_type=jnp.float32,
                    )
                    mixed = term if mixed is None else mixed + term
                picked = mixed[:BLK]
                for head in range(1, 4):
                    picked = jnp.where(lane == head, mixed[head * BLK : (head + 1) * BLK], picked)
                attended_ref[block * BLK : (block + 1) * BLK, columns] = picked.astype(jnp.bfloat16)
        projected = jnp.dot(attended_ref[...], wo_ref[...], preferred_element_type=jnp.float32)
        updated = (states_ref[member].astype(jnp.float32) + projected).astype(jnp.bfloat16)
        predicted = lax.dot_general(
            decode_ref[...], updated, (((1,), (1,)), ((), ())), preferred_element_type=jnp.float32
        )
        out_ref[member] = predicted.astype(jnp.bfloat16)


def predict(place, ids, counts, own, low, high, states, decode, mine, other):
    members, points, features = states.shape
    smem = pl.BlockSpec(memory_space=pltpu.SMEM)
    vmem = pl.BlockSpec(memory_space=pltpu.VMEM)
    blocks = 2 + 2 * REACH
    return pl.pallas_call(
        main_kernel,
        out_shape=jax.ShapeDtypeStruct((members, decode.shape[0], points), jnp.bfloat16),
        in_specs=[smem] * 3 + [vmem] * 13,
        out_specs=vmem,
        scratch_shapes=[
            pltpu.VMEM((features, 2 * HW), jnp.bfloat16),
            pltpu.VMEM((features, HW), jnp.bfloat16),
            pltpu.VMEM((HW, features), jnp.bfloat16),
            pltpu.VMEM((blocks, BLK, HW), jnp.bfloat16),
            pltpu.VMEM((blocks, BLK, HW), jnp.bfloat16),
            pltpu.VMEM((points, HW), jnp.bfloat16),
            pltpu.VMEM((points, HW), jnp.bfloat16),
        ],
        compiler_params=pltpu.CompilerParams(vmem_limit_bytes=40 << 20),
        name="predict",
    )(place, ids, counts, own, low, high, states, decode, *mine, *other)


def smooth_sign(difference):
    return difference * lax.rsqrt(difference * difference + smoothing * smoothing)


def gradient_kernel(local_ref, every_ref, targets_ref, out_ref):
    member_total = every_ref.shape[0]
    pair_weight = (1.0 - (1.0 - alpha_fair) / member_total) / (member_total - 1)
    targets = targets_ref[...].astype(jnp.float32)
    for member in range(local_ref.shape[0]):
        local = local_ref[member].astype(jnp.float32)
        pair_sum = jnp.zeros_like(local)
        for other in range(member_total):
            pair_sum += smooth_sign(local - every_ref[other].astype(jnp.float32))
        out_ref[member] = (smooth_sign(local - targets) - pair_weight * pair_sum).astype(jnp.bfloat16)


def fair_gradient(local, every, targets):
    return pl.pallas_call(
        gradient_kernel,
        out_shape=jax.ShapeDtypeStruct(local.shape, jnp.bfloat16),
        name="fair",
    )(local, every, targets)


def gather_weights(w_query, w_keyval, w_out, core):
    rows = w_query.shape[0]
    head_cols = w_query.shape[1]
    first = jnp.concatenate([w_query, w_keyval[:, :head_cols]], axis=1)
    folded = jnp.concatenate([w_out[:, :head_cols], w_out[:, head_cols:]], axis=0)
    second = jnp.concatenate([w_keyval[:, head_cols:], folded], axis=1)
    unit = jnp.where(core == 0, first, second)

    line = [unit] + [shift(unit, "yy", step) for step in (1, 3, 2)]
    line = jnp.stack([line[0], line[1], line[3], line[2]])
    y = lax.axis_index("grid") % 4
    line = lax.dynamic_slice_in_dim(jnp.concatenate([line, line]), (4 - y) % 4, 4)
    halves = line[:, :, head_cols:].reshape(4, 2, rows // 2, head_cols)
    halves = halves.transpose(1, 0, 2, 3).reshape(4, rows, head_cols)
    halves = jnp.where(core == 0, line[:, :, head_cols:], halves)
    line = jnp.concatenate([line[:, :, :head_cols], halves], axis=2)
    line = line.reshape(4 * rows, 2 * head_cols)

    by_step = {0: line}
    for step in (1, 3, 2):
        by_step[step] = shift(line, "zx", step)
    plane = jnp.stack([by_step[step] for step in range(4)])

    mine = {0: plane}
    other = {0: swap_cores(plane)}
    for step in (1, 3, 2):
        mine[step] = shift(plane, "xz", step)
        other[step] = swap_cores(mine[step])
    return [mine[step] for step in range(4)], [other[step] for step in range(4)]


def body(states, gain, w_query, w_keyval, w_out, w_decode, neighbours, counts, targets):
    member_count, points, features = states.shape
    block_count = points // BLK
    grid_size = lax.axis_size("grid")
    grid_at = lax.axis_index("grid")
    core = lax.axis_index("ens") % 2

    mine, other = gather_weights(w_query, w_keyval, w_out, core)
    normed = layer_norm(states.reshape(-1, features), gain).reshape(states.shape)
    low = lax.ppermute(normed, "grid", [(i, (i + 1) % grid_size) for i in range(grid_size)])
    high = lax.ppermute(normed, "grid", [((i + 1) % grid_size, i) for i in range(grid_size)])

    block_total = block_count * grid_size
    local_ids = (neighbours - grid_at * block_count + REACH) % block_total
    place = jnp.stack([grid_at // 16, (grid_at // 4) % 4, core]).astype(jnp.int32)
    local = predict(
        place, local_ids.reshape(-1), counts, normed, low, high, states, w_decode, mine, other
    )
    every = lax.all_gather(local, "ens", axis=0, tiled=True)
    return fair_gradient(local, every, targets).transpose(1, 0, 2)


def solution(mesh):
    in_specs = (
        P("ens", "grid", None),
        P(),
        P("grid", None),
        P("grid", None),
        P("grid", None),
        P(),
        P("grid", None),
        P("grid"),
        P(None, "grid"),
    )
    out_specs = P(None, "ens", "grid")
    return jax.shard_map(body, mesh=mesh, in_specs=in_specs, out_specs=out_specs, check_vma=False)
```
